256 devices in a mesh: grp: 8 (over z_lo, core), slab: 32 (over z_hi, x, y).
Axes of the slice: x: 4, y: 4, z: 8 (z_hi: 2, z_lo: 4; z = z_hi * 4 + z_lo), core: 2. Of those that a mesh axis runs over, the one named last changes fastest.
Arguments:
- occ_orbitals: bfloat16 [1024, 64, 4096], P(('grp', 'slab')), may hold values from -6 to 6
- vir_orbitals: bfloat16 [2048, 64, 4096], P(('grp', 'slab')), may hold values from -6 to 6
- pair_occ: int32 [8192], P(('grp', 'slab')), may hold values from 0 to 3
- pair_vir: int32 [8192], P(('grp', 'slab')), may hold values from 0 to 7
- sketch: bfloat16 [8192, 1024], P('grp'), may hold values from -6 to 6
Outputs:
- vertex: float32 [8192, 1024], P(('grp', 'slab'))
The draws below stay inside these ranges and needn't reach their ends.
Inputs may be any that keep to these rules, and one draw needn't show every extreme that they name: `pair_occ`: an index into the 4 occupied orbitals held by the same device as the pair. `pair_vir`: an index into the 8 virtual orbitals held by the same device as the pair.
All inputs are finite; a program needn't handle non-finite values.
Results may differ from the reference program's by a relative error of at most 0.0057.
Values may be sent and summed in bfloat16 or wider, within the bound.
No kernel may reach another device: no remote copies, remote signals or barrier semaphores. Data moves between devices by JAX's collectives and lax.ppermute only.
A program may use at most 192 MiB of HBM per device.

```python
import math
import jax
import jax.numpy as jnp
from jax import lax

GRID = 64
KYZ = 32
AUX = 1024
PAIR_DEV = 32
OCC_DEV = 4
VIR_DEV = 8
NCOEF = 65536
PAIRS = 8192
OCC_ALL = 1024
VIR_ALL = 2048
N_GRP = 8
N_SLAB = 32


def with_ends(values, stream_key, smallest, high):
    dims = values.shape
    place = [jax.random.randint(jax.random.fold_in(stream_key, axis), (), 0, dims[axis]) for axis in range(len(dims))]
    values = values.at[tuple(place)].set(smallest)
    longest = dims.index(max(dims))
    place[longest] = (place[longest] + 1) % dims[longest]
    return values.at[tuple(place)].set(high)


def shard_levels(own_key, extent, shards, low, high):
    gain, own = 1.0, jax.random.fold_in(own_key, 6)
    for axis_at, parts in shards:
        steps = jnp.exp(jax.random.uniform(jax.random.fold_in(own, axis_at), (parts,), jnp.float32, low / len(shards), high / len(shards)))
        gain = gain * jnp.repeat(steps, extent[axis_at] // parts).reshape([-1 if axis == axis_at else 1 for axis in range(len(extent))])
    return gain


def noise(stream_key, shape, scale, limit, shards=(), held_as=jnp.bfloat16):
    level = shard_levels(stream_key, shape, shards, -0.22, 0.18) if shards else 1.0
    drawn = jax.random.normal(stream_key, shape, jnp.float32) * scale * level
    return jnp.minimum(jnp.maximum(drawn, -limit), limit).astype(held_as)


def setup_inputs(seed: int = 0) -> dict:
    keys = jax.random.split(jax.random.key(seed), 6)
    return {
        "occ_orbitals": noise(keys[0], (OCC_ALL, GRID, GRID * GRID), 1.0, 6.0, ((0, 256),)),
        "vir_orbitals": noise(keys[1], (VIR_ALL, GRID, GRID * GRID), 1.0, 6.0, ((0, 256),)),
        "pair_occ": with_ends(jax.random.randint(keys[2], (PAIRS,), 0, OCC_DEV), jax.random.fold_in(keys[2], 1), 0, OCC_DEV - 1).astype(jnp.int32),
        "pair_vir": with_ends(jax.random.randint(keys[3], (PAIRS,), 0, VIR_DEV), jax.random.fold_in(keys[3], 1), 0, VIR_DEV - 1).astype(jnp.int32),
        "sketch": noise(keys[4], (PAIRS, AUX), 1.0, 6.0, ((0, 8),)),
    }


box_length = 10.0
screening = 1.0
epsilon = 1e-06

def real_basis(points, mode_count):
    grid_cells = jnp.arange(points, dtype=jnp.float32)[:, None]
    mode_index = jnp.arange(mode_count, dtype=jnp.int32)[None, :]
    frequency = (mode_index + 1) // 2
    phases = 2.0 * math.pi * grid_cells * frequency.astype(jnp.float32) / points
    values = jnp.where((mode_index % 2 == 1) | (mode_index == 0), jnp.cos(phases), jnp.sin(phases))
    factor = jnp.where((mode_index == 0) | (2 * frequency == points), math.sqrt(1.0 / points), math.sqrt(2.0 / points))
    return (values * factor).astype(jnp.bfloat16)

def coulomb_weight(modes_x, plane_count):
    freq_x = ((jnp.arange(modes_x, dtype=jnp.int32) + 1) // 2).astype(jnp.float32)
    freq_p = ((jnp.arange(plane_count, dtype=jnp.int32) + 1) // 2).astype(jnp.float32)
    plane_sq = (freq_p[:, None] * freq_p[:, None] + freq_p[None, :] * freq_p[None, :]).reshape(-1)
    summed_sq = plane_sq[:, None, None] + (freq_x * freq_x)[None, None, :]
    wave_sq = (2.0 * math.pi / box_length) ** 2 * summed_sq
    return jnp.sqrt(4.0 * math.pi / (wave_sq + screening * screening))

def pair_coefficients(occ_rows, vir_rows):
    pairs_dev = occ_rows.shape[0]
    grid_size = occ_rows.shape[1]
    basis_x = real_basis(grid_size, grid_size).astype(jnp.float32)
    basis_plane = real_basis(grid_size, KYZ).astype(jnp.float32)
    density = (occ_rows.astype(jnp.float32) * vir_rows.astype(jnp.float32)).astype(jnp.bfloat16)
    along_x = jnp.einsum('pxs,xk->pks', density.astype(jnp.float32), basis_x).astype(jnp.bfloat16)
    planes = along_x.reshape(pairs_dev * grid_size, grid_size, grid_size)
    second = jnp.einsum('ayz,zc->cya', planes.astype(jnp.float32), basis_plane).astype(jnp.bfloat16)
    along_y = jnp.einsum('cya,yb->bca', second.astype(jnp.float32), basis_plane)
    weighted = along_y.reshape(KYZ * KYZ, pairs_dev, grid_size) * coulomb_weight(grid_size, KYZ)
    return weighted.astype(jnp.bfloat16)

def reference(occ_orbitals, vir_orbitals, pair_occ, pair_vir, sketch):
    devices = N_GRP * N_SLAB

    def device_block(device):
        occ_table = lax.dynamic_slice_in_dim(occ_orbitals, device * OCC_DEV, OCC_DEV, 0)
        vir_table = lax.dynamic_slice_in_dim(vir_orbitals, device * VIR_DEV, VIR_DEV, 0)
        occ_ids = lax.dynamic_slice_in_dim(pair_occ, device * PAIR_DEV, PAIR_DEV, 0)
        vir_ids = lax.dynamic_slice_in_dim(pair_vir, device * PAIR_DEV, PAIR_DEV, 0)
        return pair_coefficients(occ_table[occ_ids], vir_table[vir_ids])
    gamma_all = lax.map(device_block, jnp.arange(devices, dtype=jnp.int32))
    plane_modes = KYZ * KYZ
    plane_block = math.gcd(plane_modes, 32)
    blocks = plane_modes // plane_block
    sketch_all = sketch.astype(jnp.float32).reshape(devices, PAIR_DEV, AUX)

    def sketch_block(number):
        gamma_piece = lax.dynamic_slice_in_dim(gamma_all, number * plane_block, plane_block, 1).astype(jnp.float32)
        return jnp.einsum('dypk,dpf->ykf', gamma_piece, sketch_all)
    sketch_sum = lax.map(sketch_block, jnp.arange(blocks, dtype=jnp.int32)).reshape(plane_modes, GRID, AUX)
    squares = lax.optimization_barrier(jnp.sum(sketch_sum * sketch_sum, axis=(0, 1))) / NCOEF
    field_scale = lax.rsqrt(squares + epsilon)
    field_basis = (sketch_sum * field_scale).astype(jnp.bfloat16)

    def vertex_block(running, number):
        gamma_piece = lax.dynamic_slice_in_dim(gamma_all, number * plane_block, plane_block, 1).astype(jnp.float32)
        basis_piece = lax.dynamic_slice_in_dim(field_basis, number * plane_block, plane_block, 0).astype(jnp.float32)
        return (running + jnp.einsum('dypk,ykf->dpf', gamma_piece, basis_piece), None)
    start_value = jnp.zeros((devices, PAIR_DEV, AUX), jnp.float32)
    running = lax.scan(vertex_block, start_value, jnp.arange(blocks, dtype=jnp.int32))[0]
    return (running * (1.0 / math.sqrt(NCOEF))).reshape(PAIRS, AUX)
```

```python
import math

import jax
import jax.numpy as jnp
import numpy as np
from jax import lax
from jax.sharding import Mesh, PartitionSpec as P

GRID = 64
KYZ = 32
box_length = 10.0
screening = 1.0
epsilon = 1e-06
PLANE = ("core", "x", "y")
RING = ("z_hi", "z_lo")


def real_basis(points, mode_count):
    cell = np.arange(points, dtype=np.float32)[:, None]
    mode = np.arange(mode_count, dtype=np.int32)[None, :]
    freq = (mode + 1) // 2
    phases = 2.0 * math.pi * cell * freq.astype(np.float32) / points
    values = np.where((mode % 2 == 1) | (mode == 0), np.cos(phases), np.sin(phases))
    factor = np.where((mode == 0) | (2 * freq == points), math.sqrt(1.0 / points), math.sqrt(2.0 / points))
    return jnp.asarray((values * factor).astype(np.float32)).astype(jnp.bfloat16)


def coulomb_weight(modes_x, modes_p):
    freq_x = ((jnp.arange(modes_x, dtype=jnp.int32) + 1) // 2).astype(jnp.float32)
    freq_p = ((jnp.arange(modes_p, dtype=jnp.int32) + 1) // 2).astype(jnp.float32)
    plane_sq = (freq_p[:, None] * freq_p[:, None] + freq_p[None, :] * freq_p[None, :]).reshape(-1)
    summed_sq = (freq_x * freq_x)[:, None] + plane_sq[None, :]
    wave_sq = (2.0 * math.pi / box_length) ** 2 * summed_sq
    return jnp.sqrt(4.0 * math.pi / (wave_sq + screening * screening))


def body(occ_orbitals, vir_orbitals, pair_occ, pair_vir, sketch):
    pairs = pair_occ.shape[0]
    fields = sketch.shape[1]
    coef_count = GRID * KYZ * KYZ
    f32 = jnp.float32
    mine = sketch.reshape(2, -1, fields)[lax.axis_index("z_hi")]
    sketch_plane = lax.all_gather(mine, "core", axis=0, tiled=True)

    basis_x = real_basis(GRID, GRID)
    basis_p = real_basis(GRID, KYZ)
    density = (occ_orbitals[pair_occ] * vir_orbitals[pair_vir]).reshape(pairs * GRID, GRID * GRID)
    kron_yz = (basis_p.astype(f32)[:, None, :, None] * basis_p.astype(f32)[None, :, None, :]).reshape(
        GRID * GRID, KYZ * KYZ
    ).astype(jnp.bfloat16)
    second = jnp.dot(density, kron_yz, preferred_element_type=f32).astype(jnp.bfloat16)
    half = 16
    eye = jnp.eye(half, dtype=jnp.bfloat16)
    mix_x = (basis_x.T[:, None, None, :] * eye[None, :, :, None]).reshape(GRID * half, half * GRID)
    blocks = second.reshape(pairs // half, half * GRID, KYZ * KYZ)
    weight = coulomb_weight(GRID, KYZ)
    parts = []
    for h in range(pairs // half):
        along = jnp.dot(mix_x, blocks[h], preferred_element_type=f32).reshape(GRID, half, KYZ * KYZ)
        parts.append((along * weight[:, None, :]).astype(jnp.bfloat16))
    gamma = jnp.concatenate(parts, axis=1)

    slabs = gamma.reshape(32, 2, pairs, KYZ * KYZ)
    received, terms = [], []
    for h in range(2):
        got = lax.all_to_all(slabs[:, h], PLANE, split_axis=0, concat_axis=0, tiled=True)
        got = got.reshape(32 * pairs, KYZ * KYZ)
        received.append(got)
        part = lax.dot_general(sketch_plane, got, (((0,), (0,)), ((), ())), preferred_element_type=f32)
        part = part.astype(jnp.bfloat16)
        mine_sum = lax.psum_scatter(part, RING, scatter_dimension=0, tiled=True)
        whole = lax.all_gather(mine_sum, RING, axis=0, tiled=True)
        terms.append(whole)
    squares = sum(jnp.sum(jnp.square(t.astype(f32)), axis=1) for t in terms)
    vertex = sum(
        lax.dot_general(g, t, (((1,), (1,)), ((), ())), preferred_element_type=f32)
        for g, t in zip(received, terms)
    ).astype(jnp.bfloat16)
    all_squares = lax.all_gather(squares[None], PLANE, axis=0, tiled=True)
    scale = lax.rsqrt(jnp.sum(all_squares, axis=0) / coef_count + epsilon) * (1.0 / math.sqrt(coef_count))
    shares = lax.all_to_all(vertex.reshape(32, pairs, fields), PLANE, split_axis=0, concat_axis=0, tiled=True)
    return jnp.sum(shares.astype(f32), axis=0) * scale[None, :]


def solution(mesh):
    wide = Mesh(mesh.devices.reshape(4, 2, 2, 4, 4), ("z_lo", "core", "z_hi", "x", "y"))
    whole = ("z_lo", "core", "z_hi", "x", "y")
    return jax.shard_map(
        body,
        mesh=wide,
        in_specs=(P(whole), P(whole), P(whole), P(whole), P(("z_lo", "core"))),
        out_specs=P(whole),
        check_vma=False,
    )
```

```python
import math

import jax
import jax.numpy as jnp
import numpy as np
from jax import lax
from jax.experimental import pallas as pl
from jax.experimental.pallas import tpu as pltpu
from jax.sharding import Mesh, PartitionSpec as P

GRID = 64
KYZ = 32
box_length = 10.0
screening = 1.0
epsilon = 1e-06
PLANE = ("core", "x", "y")
RING = ("z_hi", "z_lo")
BLOCK = 8
YGRP = 8
HALF = 16
f32 = jnp.float32
bf16 = jnp.bfloat16


def real_basis(points, mode_count):
    cell = np.arange(points, dtype=np.float32)[:, None]
    mode = np.arange(mode_count, dtype=np.int32)[None, :]
    freq = (mode + 1) // 2
    phases = 2.0 * math.pi * cell * freq.astype(np.float32) / points
    values = np.where((mode % 2 == 1) | (mode == 0), np.cos(phases), np.sin(phases))
    factor = np.where((mode == 0) | (2 * freq == points), math.sqrt(1.0 / points), math.sqrt(2.0 / points))
    return (values * factor).astype(np.float32)


def constants():
    basis_x = real_basis(GRID, GRID)
    basis_p = real_basis(GRID, KYZ)
    eye_y = np.eye(YGRP, dtype=np.float32)
    eye_k = np.eye(HALF, dtype=np.float32)
    eye_p = np.eye(BLOCK, dtype=np.float32)
    split = basis_p.reshape(GRID, 2, HALF)
    along_z = np.einsum("yw,zqk->yzqwk", eye_y, split).reshape(YGRP * GRID, YGRP * KYZ)
    along_y = np.einsum("yb,km->ykbm", basis_p, eye_k).reshape(GRID * HALF, KYZ * HALF)
    along_x = np.einsum("xk,pr->kprx", basis_x, eye_p).reshape(GRID * BLOCK, BLOCK * GRID)
    freq_x = ((np.arange(GRID) + 1) // 2).astype(np.float32)
    freq_p = ((np.arange(KYZ) + 1) // 2).astype(np.float32)
    freq_q = freq_p.reshape(2, HALF)
    square = (
        (freq_x**2)[:, None, None, None]
        + (freq_p**2)[None, None, :, None]
        + (freq_q**2)[None, :, None, :]
    ).astype(np.float32)
    wave = np.float32((2.0 * math.pi / box_length) ** 2) * square
    weight = np.sqrt(np.float32(4.0 * math.pi) / (wave + np.float32(screening * screening)))
    weight = weight.reshape(GRID, 1, KYZ * KYZ).astype(np.float32)
    return (
        jnp.asarray(along_z).astype(bf16),
        jnp.asarray(along_y).astype(bf16),
        jnp.asarray(along_x).astype(bf16),
        jnp.asarray(weight),
    )


def gamma_kernel(po, pv, occ, vir, along_z, along_y, along_x, weight, out, dens, first, second):
    step = pl.program_id(0)
    rows = BLOCK * GRID
    tile_in = YGRP * GRID
    tile_out = YGRP * HALF
    width = KYZ * HALF
    for r in range(BLOCK):
        o = po[step * BLOCK + r]
        v = pv[step * BLOCK + r]
        dens[r * GRID : (r + 1) * GRID, :] = occ[o] * vir[v]
    for j in range(GRID // YGRP):
        t = jnp.dot(dens[:, j * tile_in : (j + 1) * tile_in], along_z[...], preferred_element_type=f32).astype(bf16)
        first[0, :, j * tile_out : (j + 1) * tile_out] = t[:, :tile_out]
        first[1, :, j * tile_out : (j + 1) * tile_out] = t[:, tile_out:]
    for q in range(2):
        second[:, q * width : (q + 1) * width] = jnp.dot(
            first[q], along_y[...], preferred_element_type=f32
        ).astype(bf16)
    piece = 256
    plane = KYZ * KYZ
    for n in range(plane // piece):
        g = jnp.dot(along_x[...], second[:, n * piece : (n + 1) * piece], preferred_element_type=f32)
        g = g.reshape(GRID, BLOCK, piece) * weight[:, :, n * piece : (n + 1) * piece]
        g = g.astype(bf16).reshape(GRID // 2, 2, BLOCK, piece)
        out[:, :, n * piece : (n + 1) * piece] = g[:, 0]
        out[:, :, plane + n * piece : plane + (n + 1) * piece] = g[:, 1]


def make_gamma(occ, vir, pair_occ, pair_vir):
    pairs = pair_occ.shape[0]
    along_z, along_y, along_x, weight = constants()
    rows = BLOCK * GRID
    full = lambda shape: pl.BlockSpec(shape, lambda i, a, b: (0,) * len(shape), pipeline_mode=pl.Buffered(1))
    return pl.pallas_call(
        gamma_kernel,
        out_shape=jax.ShapeDtypeStruct((GRID // 2, pairs, 2 * KYZ * KYZ), bf16),
        grid_spec=pltpu.PrefetchScalarGridSpec(
            num_scalar_prefetch=2,
            grid=(pairs // BLOCK,),
            in_specs=[
                full(occ.shape),
                full(vir.shape),
                full(along_z.shape),
                full(along_y.shape),
                full(along_x.shape),
                full(weight.shape),
            ],
            out_specs=pl.BlockSpec((GRID // 2, BLOCK, 2 * KYZ * KYZ), lambda i, a, b: (0, i, 0)),
            scratch_shapes=[
                pltpu.VMEM((rows, GRID * GRID), bf16),
                pltpu.VMEM((2, rows, GRID * HALF), bf16),
                pltpu.VMEM((rows, KYZ * KYZ), bf16),
            ],
        ),
        cost_estimate=pl.CostEstimate(flops=11_000_000_000, bytes_accessed=14_000_000, transcendentals=0),
        name="gamma",
    )(pair_occ, pair_vir, occ, vir, along_z, along_y, along_x, weight)


def body(occ_orbitals, vir_orbitals, pair_occ, pair_vir, sketch):
    pairs = pair_occ.shape[0]
    fields = sketch.shape[1]
    coef_count = GRID * KYZ * KYZ
    mine = sketch.reshape(2, -1, fields)[lax.axis_index("z_hi")]
    sketch_plane = lax.all_gather(mine, "core", axis=0, tiled=True)

    gamma = make_gamma(occ_orbitals, vir_orbitals, pair_occ, pair_vir)
    got = lax.all_to_all(gamma, PLANE, split_axis=0, concat_axis=0, tiled=True)
    got = got.reshape(32 * pairs, -1)
    part = lax.dot_general(sketch_plane, got, (((0,), (0,)), ((), ())), preferred_element_type=f32)
    mine_sum = lax.psum_scatter(part.astype(bf16), RING, scatter_dimension=0, tiled=True)
    whole = lax.all_gather(mine_sum, RING, axis=0, tiled=True)
    squares = jnp.sum(jnp.square(mine_sum.astype(f32)), axis=1)
    spread = jnp.broadcast_to(squares[None, None, :], (32, 8, squares.shape[0]))
    squares = jnp.sum(lax.all_to_all(spread, PLANE, split_axis=0, concat_axis=0, tiled=True)[:, 0, :], axis=0)
    scale = lax.rsqrt(squares / coef_count + epsilon) * (1.0 / math.sqrt(coef_count))
    spread = jnp.broadcast_to(scale[None, None, :], (8, 8, squares.shape[0]))
    scale = lax.all_to_all(spread, RING, split_axis=0, concat_axis=0, tiled=True)[:, 0, :].reshape(1, fields)

    vertex = lax.dot_general(got, whole, (((1,), (1,)), ((), ())), preferred_element_type=f32).astype(bf16)
    shares = lax.all_to_all(vertex.reshape(32, pairs, fields), PLANE, split_axis=0, concat_axis=0, tiled=True)
    return jnp.sum(shares.astype(f32), axis=0) * scale


def solution(mesh):
    wide = Mesh(mesh.devices.reshape(4, 2, 2, 4, 4), ("z_lo", "core", "z_hi", "x", "y"))
    whole = ("z_lo", "core", "z_hi", "x", "y")
    return jax.shard_map(
        body,
        mesh=wide,
        in_specs=(P(whole), P(whole), P(whole), P(whole), P(("z_lo", "core"))),
        out_specs=P(whole),
        check_vma=False,
    )
```

```python
import math

import jax
import jax.numpy as jnp
import numpy as np
from jax import lax
from jax.experimental import pallas as pl
from jax.experimental.pallas import tpu as pltpu
from jax.sharding import Mesh, PartitionSpec as P

GRID = 64
KYZ = 32
box_length = 10.0
screening = 1.0
epsilon = 1e-06
PLANE = ("core", "x", "y")
BLOCK = 8
YGRP = 8
HALF = 16
f32 = jnp.float32
bf16 = jnp.bfloat16


def real_basis(points, mode_count):
    cell = np.arange(points, dtype=np.float32)[:, None]
    mode = np.arange(mode_count, dtype=np.int32)[None, :]
    freq = (mode + 1) // 2
    phases = 2.0 * math.pi * cell * freq.astype(np.float32) / points
    values = np.where((mode % 2 == 1) | (mode == 0), np.cos(phases), np.sin(phases))
    factor = np.where((mode == 0) | (2 * freq == points), math.sqrt(1.0 / points), math.sqrt(2.0 / points))
    return (values * factor).astype(np.float32)


def constants():
    basis_x = real_basis(GRID, GRID)
    basis_p = real_basis(GRID, KYZ)
    eye_y = np.eye(YGRP, dtype=np.float32)
    eye_k = np.eye(HALF, dtype=np.float32)
    eye_p = np.eye(BLOCK, dtype=np.float32)
    split = basis_p.reshape(GRID, 2, HALF)
    along_z = np.einsum("yw,zqk->yzqwk", eye_y, split).reshape(YGRP * GRID, YGRP * KYZ)
    along_y = np.einsum("yb,km->ykbm", basis_p, eye_k).reshape(GRID * HALF, KYZ * HALF)
    along_x = np.einsum("xk,pr->kprx", basis_x, eye_p).reshape(GRID * BLOCK, BLOCK * GRID)
    freq_x = ((np.arange(GRID) + 1) // 2).astype(np.float32)
    freq_p = ((np.arange(KYZ) + 1) // 2).astype(np.float32)
    freq_q = freq_p.reshape(2, HALF)
    square = (
        (freq_x**2)[:, None, None, None]
        + (freq_p**2)[None, None, :, None]
        + (freq_q**2)[None, :, None, :]
    ).astype(np.float32)
    wave = np.float32((2.0 * math.pi / box_length) ** 2) * square
    weight = np.sqrt(np.float32(4.0 * math.pi) / (wave + np.float32(screening * screening)))
    weight = weight.reshape(GRID, 1, KYZ * KYZ).astype(np.float32)
    return (
        jnp.asarray(along_z).astype(bf16),
        jnp.asarray(along_y).astype(bf16),
        jnp.asarray(along_x).astype(bf16),
        jnp.asarray(weight),
    )


def gamma_kernel(po, pv, occ, vir, along_z, along_y, along_x, weight, out0, out1, dens, first, second):
    step = pl.program_id(0)
    tile_in = YGRP * GRID
    tile_out = YGRP * HALF
    width = KYZ * HALF
    for r in range(BLOCK):
        o = po[step * BLOCK + r]
        v = pv[step * BLOCK + r]
        dens[r * GRID : (r + 1) * GRID, :] = occ[o] * vir[v]
    for j in range(GRID // YGRP):
        t = jnp.dot(dens[:, j * tile_in : (j + 1) * tile_in], along_z[...], preferred_element_type=f32).astype(bf16)
        first[0, :, j * tile_out : (j + 1) * tile_out] = t[:, :tile_out]
        first[1, :, j * tile_out : (j + 1) * tile_out] = t[:, tile_out:]
    for q in range(2):
        second[:, q * width : (q + 1) * width] = jnp.dot(
            first[q], along_y[...], preferred_element_type=f32
        ).astype(bf16)
    piece = 256
    for n in range(KYZ * KYZ // piece):
        cols = slice(n * piece, (n + 1) * piece)
        g = jnp.dot(along_x[...], second[:, cols], preferred_element_type=f32)
        g = g.reshape(GRID, BLOCK, piece) * weight[:, :, cols]
        g = g.astype(bf16).reshape(GRID // 2, 2, BLOCK, piece)
        out0[:, :, cols] = g[:, 0]
        out1[:, :, cols] = g[:, 1]


def make_gamma(occ, vir, pair_occ, pair_vir):
    pairs = pair_occ.shape[0]
    plane = KYZ * KYZ
    along_z, along_y, along_x, weight = constants()
    rows = BLOCK * GRID
    full = lambda shape: pl.BlockSpec(shape, lambda i, a, b: (0,) * len(shape), pipeline_mode=pl.Buffered(1))
    half = pl.BlockSpec((GRID // 2, BLOCK, plane), lambda i, a, b: (0, i, 0))
    return pl.pallas_call(
        gamma_kernel,
        out_shape=[jax.ShapeDtypeStruct((GRID // 2, pairs, plane), bf16)] * 2,
        grid_spec=pltpu.PrefetchScalarGridSpec(
            num_scalar_prefetch=2,
            grid=(pairs // BLOCK,),
            in_specs=[
                full(occ.shape),
                full(vir.shape),
                full(along_z.shape),
                full(along_y.shape),
                full(along_x.shape),
                full(weight.shape),
            ],
            out_specs=[half, half],
            scratch_shapes=[
                pltpu.VMEM((rows, GRID * GRID), bf16),
                pltpu.VMEM((2, rows, GRID * HALF), bf16),
                pltpu.VMEM((rows, plane), bf16),
            ],
        ),
        cost_estimate=pl.CostEstimate(flops=11_000_000_000, bytes_accessed=14_000_000, transcendentals=0),
        name="gamma",
    )(pair_occ, pair_vir, occ, vir, along_z, along_y, along_x, weight)


def ring_shift(value, by):
    place = lambda z: (z % 4) * 2 + z // 4
    return lax.ppermute(value, ("z_lo", "z_hi"), [(place(z), place((z + by) % 8)) for z in range(8)])


def exchange(value):
    return lax.all_to_all(value, PLANE, split_axis=0, concat_axis=0, tiled=True)


HEAD = 3
ROWS = 8


def body(occ_orbitals, vir_orbitals, pair_occ, pair_vir, sketch):
    pairs = pair_occ.shape[0]
    fields = sketch.shape[1]
    wide = fields // 8
    coef_count = GRID * KYZ * KYZ
    z = lax.axis_index("z_hi") * 4 + lax.axis_index("z_lo")

    gammas = make_gamma(occ_orbitals, vir_orbitals, pair_occ, pair_vir)
    got = [exchange(g).reshape(32 * pairs, -1) for g in gammas]

    mine = sketch.reshape(2, -1, fields)[lax.axis_index("z_hi")]
    other = lax.ppermute(mine, "core", [(0, 1), (1, 0)])
    upper = lax.axis_index("core") == 0
    rows = jnp.concatenate([jnp.where(upper, mine, other), jnp.where(upper, other, mine)], axis=0)
    blocks = rows.T.reshape(8, wide, 32 * pairs)
    blocks = lax.dynamic_slice_in_dim(jnp.concatenate([blocks, blocks[:7]], axis=0), (z + HEAD) % 8, 8, 0)
    blocks = lax.optimization_barrier(blocks)

    squares = 0.0
    gathered = []
    for c in range(2):
        up = (3, 2, 1) if c == 0 else (4, 3, 2, 1)
        down = (4, 5, 6, 7) if c == 0 else (5, 6, 7)
        ahead = 2 if c == 0 else 3
        term = {}
        for at, to in ((0, ahead), (ahead, 8)):
            part = lax.dot_general(
                blocks[at:to].reshape((to - at) * wide, -1),
                got[c],
                (((1,), (0,)), ((), ())),
                preferred_element_type=f32,
            ).reshape(to - at, wide, -1)
            for i in range(at, to):
                term[(HEAD + i) % 8] = part[i - at]
        runs = {-1: term[down[0]].astype(bf16), 1: term[up[0]].astype(bf16)}
        for i in range(1, 4):
            for order, by in ((down, -1), (up, 1)):
                if i < len(order):
                    runs[by] = (ring_shift(runs[by], by).astype(f32) + term[order[i]]).astype(bf16)
            if c == 0 and i == 2:
                got[1] = lax.optimization_barrier((got[1], runs[1], runs[-1]))[0]
        total = term[0] + ring_shift(runs[-1], -1).astype(f32) + ring_shift(runs[1], 1).astype(f32)
        squares = squares + jnp.sum(jnp.square(total), axis=1)
        block = total.astype(bf16)
        if c == 1:
            high = squares.astype(bf16)
            low = (squares - high.astype(f32)).astype(bf16)
            tail = jnp.concatenate([high, low, jnp.zeros((block.shape[1] - 2 * wide,), bf16)])
            block = jnp.concatenate([block, jnp.broadcast_to(tail[None], (ROWS, block.shape[1]))], axis=0)
        held = {0: block}
        if c == 0:
            run = {-1: block, 1: block}
            for i in range(4):
                for by, hops in ((-1, 4), (1, 3)):
                    if i < hops:
                        run[by] = ring_shift(run[by], by)
                        held[(-by * (i + 1)) % 8] = run[by]
        else:
            for k in (7, 1, 6, 2):
                held[k] = ring_shift(block, -k if k < 4 else 8 - k)
            held[5] = ring_shift(held[6], 1)
            held[3] = ring_shift(held[2], -1)
            cut = wide // 2
            held[4] = jnp.concatenate([ring_shift(held[6][:cut], 2), ring_shift(held[2][cut:], -2)], axis=0)
        gathered.append(held)

    def product(c, group):
        side = jnp.concatenate([gathered[c][k][:wide] for k in group], axis=0)
        return lax.dot_general(got[c], side, (((1,), (1,)), ((), ())), preferred_element_type=f32)

    groups = ((6, 7, 0, 1, 2), (3, 4, 5))
    early = [product(0, group) for group in groups]
    early = list(lax.optimization_barrier(tuple(early)))
    pieces = []
    for i, group in enumerate(groups):
        pieces.append((product(1, group) + early[i]).astype(bf16).reshape(32, pairs, -1))
    tails = jnp.concatenate([gathered[1][k][wide : wide + 1, : 2 * wide] for k in (6, 7, 0, 1, 2, 3, 4, 5)], axis=0)
    extra = jnp.concatenate([tails[:, :wide], tails[:, wide:], jnp.zeros((pairs - 16, wide), bf16)], axis=0)
    extra = jnp.broadcast_to(extra[None], (32, pairs, wide))
    first = pieces[0]
    last = jnp.concatenate([pieces[1], extra], axis=2)
    first = jnp.sum(exchange(first).astype(f32), axis=0)
    last = jnp.sum(exchange(last).astype(f32), axis=0)
    rolled = jnp.concatenate([first, last[:, : 3 * wide]], axis=1).reshape(pairs, 8, wide)
    sums = last[:, 3 * wide :]
    scale = lax.rsqrt((sums[:8] + sums[8:16]) / coef_count + epsilon) * (1.0 / math.sqrt(coef_count))
    rolled = rolled * scale[None]
    rolled = jnp.concatenate([rolled, rolled], axis=1)
    return lax.dynamic_slice_in_dim(rolled, (16 - z - 6) % 8, 8, 1).reshape(pairs, fields)


def solution(mesh):
    wide = Mesh(mesh.devices.reshape(4, 2, 2, 4, 4), ("z_lo", "core", "z_hi", "x", "y"))
    whole = ("z_lo", "core", "z_hi", "x", "y")

    return jax.shard_map(
        body,
        mesh=wide,
        in_specs=(P(whole), P(whole), P(whole), P(whole), P(("z_lo", "core"))),
        out_specs=P(whole),
        check_vma=False,
    )
```

```python
import math

import jax
import jax.numpy as jnp
import numpy as np
from jax import lax
from jax.experimental import pallas as pl
from jax.experimental.pallas import tpu as pltpu
from jax.sharding import Mesh, PartitionSpec as P

GRID = 64
KYZ = 32
box_length = 10.0
screening = 1.0
epsilon = 1e-06
PLANE = ("core", "x", "y")
BLOCK = 8
YGRP = 8
HALF = 16
f32 = jnp.float32
bf16 = jnp.bfloat16


def real_basis(points, mode_count):
    cell = np.arange(points, dtype=np.float32)[:, None]
    mode = np.arange(mode_count, dtype=np.int32)[None, :]
    freq = (mode + 1) // 2
    phases = 2.0 * math.pi * cell * freq.astype(np.float32) / points
    values = np.where((mode % 2 == 1) | (mode == 0), np.cos(phases), np.sin(phases))
    factor = np.where((mode == 0) | (2 * freq == points), math.sqrt(1.0 / points), math.sqrt(2.0 / points))
    return (values * factor).astype(np.float32)


def weights():
    freq_x = ((np.arange(GRID) + 1) // 2).astype(np.float32)
    freq_p = ((np.arange(KYZ) + 1) // 2).astype(np.float32)
    freq_q = freq_p.reshape(2, HALF)
    square = (
        (freq_x**2)[None, :, None, None] + (freq_p**2)[None, None, :, None] + (freq_q**2)[:, None, None, :]
    ).astype(np.float32)
    wave = np.float32((2.0 * math.pi / box_length) ** 2) * square
    weight = np.sqrt(np.float32(4.0 * math.pi) / (wave + np.float32(screening * screening)))
    return weight.reshape(2, GRID, 1, KYZ * HALF).astype(np.float32)


def spread(small, shape, row_of, col_of, keep):
    one_hot = lambda hit: jnp.where(hit, 1.0, 0.0).astype(bf16)
    iota = lambda dims, dim: lax.broadcasted_iota(jnp.int32, dims, dim)
    tall = (shape[0], small.shape[0])
    flat = (small.shape[1], shape[1])
    left = one_hot(row_of(iota(tall, 0)) == iota(tall, 1))
    right = one_hot(iota(flat, 0) == col_of(iota(flat, 1)))
    mid = jnp.dot(left, small, preferred_element_type=f32).astype(bf16)
    whole = jnp.dot(mid, right, preferred_element_type=f32)
    return jnp.where(keep(iota(shape, 0), iota(shape, 1)), whole, 0.0).astype(bf16)


def later_matrices(basis_x, basis_p, along_y, along_x):
    along_y[...] = spread(
        basis_p[...], along_y.shape, lambda r: r >> 4, lambda c: c >> 4, lambda r, c: (r & 15) == (c & 15)
    )
    along_x[...] = spread(
        basis_x[...], along_x.shape, lambda r: r >> 3, lambda c: c & 63, lambda r, c: (r & 7) == (c >> 6)
    )


def finish(first, along_y, along_x, weight, out):
    width = KYZ * HALF
    second = jnp.dot(first, along_y[...], preferred_element_type=f32).astype(bf16)
    piece = 256
    for n in range(width // piece):
        cols = slice(n * piece, (n + 1) * piece)
        g = jnp.dot(along_x[...], second[:, cols], preferred_element_type=f32)
        g = g.reshape(GRID, BLOCK, piece) * weight[:, :, cols]
        g = g.astype(bf16).reshape(GRID // 2, 2, BLOCK, piece)
        out[:, :, cols] = g[:, 0]
        out[:, :, width + n * piece : width + (n + 1) * piece] = g[:, 1]


def first_kernel(
    po, pv, occ_hbm, vir_hbm, basis_x, basis_p, weight, out, rest, occ, vir, dens, first, along_z, along_y, along_x, sems
):
    step = pl.program_id(0)

    @pl.when(step == 0)
    def _():
        loads = [
            pltpu.make_async_copy(occ_hbm, occ, sems.at[0]),
            pltpu.make_async_copy(vir_hbm, vir, sems.at[1]),
        ]
        for load in loads:
            load.start()
        along_z[...] = spread(
            basis_p[...],
            along_z.shape,
            lambda r: r & 63,
            lambda c: ((c >> 7) << 4) + (c & 15),
            lambda r, c: (r >> 6) == ((c & 127) >> 4),
        )
        later_matrices(basis_x, basis_p, along_y, along_x)
        for load in loads:
            load.wait()

    tile_in = YGRP * GRID
    tile_out = YGRP * HALF
    for r in range(BLOCK):
        o = po[step * BLOCK + r]
        v = pv[step * BLOCK + r]
        dens[r * GRID : (r + 1) * GRID, :] = occ[o] * vir[v]
    for j in range(GRID // YGRP):
        t = jnp.dot(dens[:, j * tile_in : (j + 1) * tile_in], along_z[...], preferred_element_type=f32).astype(bf16)
        first[:, j * tile_out : (j + 1) * tile_out] = t[:, :tile_out]
        rest[:, j * tile_out : (j + 1) * tile_out] = t[:, tile_out:]
    finish(first[...], along_y, along_x, weight, out)


def second_kernel(first, basis_x, basis_p, weight, out, along_y, along_x):
    @pl.when(pl.program_id(0) == 0)
    def _():
        later_matrices(basis_x, basis_p, along_y, along_x)

    finish(first[...], along_y, along_x, weight, out)


def make_gamma(occ, vir, pair_occ, pair_vir):
    pairs = pair_occ.shape[0]
    plane = KYZ * KYZ
    rows = BLOCK * GRID
    steps = pairs // BLOCK
    basis_x = jnp.asarray(real_basis(GRID, GRID).T).astype(bf16)
    basis_p = jnp.asarray(real_basis(GRID, KYZ)).astype(bf16)
    weight = weights()
    full = lambda shape: pl.BlockSpec(shape, lambda *at: (0,) * len(shape), pipeline_mode=pl.Buffered(1))
    half = pl.BlockSpec((GRID // 2, BLOCK, plane), lambda i, *_: (0, i, 0))
    part = pl.BlockSpec((rows, GRID * HALF), lambda i, *_: (i, 0))
    out_shape = jax.ShapeDtypeStruct((GRID // 2, pairs, plane), bf16)
    matrices = [pltpu.VMEM((GRID * HALF, KYZ * HALF), bf16), pltpu.VMEM((rows, rows), bf16)]
    front, rest = pl.pallas_call(
        first_kernel,
        out_shape=[out_shape, jax.ShapeDtypeStruct((pairs * GRID, GRID * HALF), bf16)],
        grid_spec=pltpu.PrefetchScalarGridSpec(
            num_scalar_prefetch=2,
            grid=(steps,),
            in_specs=[
                pl.BlockSpec(memory_space=pl.ANY),
                pl.BlockSpec(memory_space=pl.ANY),
                full(basis_x.shape),
                full(basis_p.shape),
                full(weight[0].shape),
            ],
            out_specs=[half, part],
            scratch_shapes=[
                pltpu.VMEM(occ.shape, bf16),
                pltpu.VMEM(vir.shape, bf16),
                pltpu.VMEM((rows, GRID * GRID), bf16),
                pltpu.VMEM((rows, GRID * HALF), bf16),
                pltpu.VMEM((YGRP * GRID, YGRP * KYZ), bf16),
                *matrices,
                pltpu.SemaphoreType.DMA((2,)),
            ],
        ),
        cost_estimate=pl.CostEstimate(flops=8_000_000_000, bytes_accessed=12_000_000, transcendentals=0),
        name="gamma_first",
    )(pair_occ, pair_vir, occ, vir, basis_x, basis_p, jnp.asarray(weight[0]))
    back = pl.pallas_call(
        second_kernel,
        out_shape=out_shape,
        grid_spec=pl.GridSpec(
            grid=(steps,),
            in_specs=[part, full(basis_x.shape), full(basis_p.shape), full(weight[1].shape)],
            out_specs=half,
            scratch_shapes=matrices,
        ),
        cost_estimate=pl.CostEstimate(flops=4_000_000_000, bytes_accessed=6_000_000, transcendentals=0),
        name="gamma_second",
    )(rest, basis_x, basis_p, jnp.asarray(weight[1]))
    return [front, back]


def ring_shift(value, by):
    place = lambda z: (z % 4) * 2 + z // 4
    return lax.ppermute(value, ("z_lo", "z_hi"), [(place(z), place((z + by) % 8)) for z in range(8)])


def exchange(value):
    return lax.all_to_all(value, PLANE, split_axis=0, concat_axis=0, tiled=True)


HEAD = 3
ROWS = 8


def body(occ_orbitals, vir_orbitals, pair_occ, pair_vir, sketch):
    pairs = pair_occ.shape[0]
    fields = sketch.shape[1]
    wide = fields // 8
    coef_count = GRID * KYZ * KYZ
    z = lax.axis_index("z_hi") * 4 + lax.axis_index("z_lo")

    gammas = make_gamma(occ_orbitals, vir_orbitals, pair_occ, pair_vir)
    got = [exchange(g).reshape(32 * pairs, -1) for g in gammas]

    mine = sketch.reshape(2, -1, fields)[lax.axis_index("z_hi")]
    other = lax.ppermute(mine, "core", [(0, 1), (1, 0)])
    upper = lax.axis_index("core") == 0
    rows = jnp.concatenate([jnp.where(upper, mine, other), jnp.where(upper, other, mine)], axis=0)
    blocks = rows.T.reshape(8, wide, 32 * pairs)
    blocks = lax.dynamic_slice_in_dim(jnp.concatenate([blocks, blocks[:7]], axis=0), (z + HEAD) % 8, 8, 0)
    blocks = lax.optimization_barrier(blocks)

    squares = 0.0
    gathered = []
    for c in range(2):
        up = (3, 2, 1) if c == 0 else (4, 3, 2, 1)
        down = (4, 5, 6, 7) if c == 0 else (5, 6, 7)
        ahead = 2 if c == 0 else 3
        term = {}
        for at, to in ((0, ahead), (ahead, 8)):
            part = lax.dot_general(
                blocks[at:to].reshape((to - at) * wide, -1),
                got[c],
                (((1,), (0,)), ((), ())),
                preferred_element_type=f32,
            ).reshape(to - at, wide, -1)
            for i in range(at, to):
                term[(HEAD + i) % 8] = part[i - at]
        runs = {-1: term[down[0]].astype(bf16), 1: term[up[0]].astype(bf16)}
        for i in range(1, 4):
            for order, by in ((down, -1), (up, 1)):
                if i < len(order):
                    runs[by] = (ring_shift(runs[by], by).astype(f32) + term[order[i]]).astype(bf16)
            if c == 0 and i == 2:
                got[1] = lax.optimization_barrier((got[1], runs[1], runs[-1]))[0]
        total = term[0] + ring_shift(runs[-1], -1).astype(f32) + ring_shift(runs[1], 1).astype(f32)
        squares = squares + jnp.sum(jnp.square(total), axis=1)
        block = total.astype(bf16)
        if c == 1:
            high = squares.astype(bf16)
            low = (squares - high.astype(f32)).astype(bf16)
            tail = jnp.concatenate([high, low, jnp.zeros((block.shape[1] - 2 * wide,), bf16)])
            block = jnp.concatenate([block, jnp.broadcast_to(tail[None], (ROWS, block.shape[1]))], axis=0)
        held = {0: block}
        run = {-1: block, 1: block}
        for i in range(4):
            for by, hops in ((-1, 4 if c == 0 else 3), (1, 3 if c == 0 else 4)):
                if i < hops:
                    run[by] = ring_shift(run[by], by)
                    held[(-by * (i + 1)) % 8] = run[by]
        gathered.append(held)

    def product(c):
        side = jnp.concatenate([gathered[c][k][:wide] for k in range(8)], axis=0)
        return lax.dot_general(got[c], side, (((1,), (1,)), ((), ())), preferred_element_type=f32)

    early = product(0)
    early = lax.optimization_barrier(early)
    vertex = (product(1) + early).astype(bf16)
    tails = [gathered[1][k][wide : wide + 1, : 2 * wide] for k in range(8)]
    sums = jnp.concatenate([t[:, :wide] for t in tails], axis=1), jnp.concatenate([t[:, wide:] for t in tails], axis=1)
    sums = jnp.concatenate([*sums, jnp.zeros((ROWS - 2, fields), bf16)], axis=0)
    half = 16 * pairs
    place = lax.axis_index("core")
    away = lax.dynamic_slice_in_dim(vertex, (1 - place) * half, half, 0)
    away = lax.ppermute(jnp.concatenate([away, sums], axis=0), "core", [(0, 1), (1, 0)])
    near = lax.dynamic_slice_in_dim(vertex, place * half, half, 0)
    both = (near.astype(f32) + away[:half].astype(f32)).astype(bf16).reshape(16, pairs, fields)
    total = sums.astype(f32) + away[half:].astype(f32)
    total = total[:1] + total[1:2]
    high = total.astype(bf16)
    low = (total - high.astype(f32)).astype(bf16)
    total = jnp.concatenate([high, low, jnp.zeros((ROWS - 2, fields), bf16)], axis=0)
    both = jnp.concatenate([both, jnp.broadcast_to(total[None], (16, ROWS, fields))], axis=1)
    shares = lax.all_to_all(both, ("x", "y"), split_axis=0, concat_axis=0, tiled=True)
    shares = jnp.sum(shares.astype(f32), axis=0)
    scale = lax.rsqrt((shares[pairs : pairs + 1] + shares[pairs + 1 : pairs + 2]) / coef_count + epsilon)
    rolled = shares[:pairs] * (scale * (1.0 / math.sqrt(coef_count)))
    rolled = jnp.concatenate([rolled, rolled], axis=1)
    return lax.dynamic_slice_in_dim(rolled, (8 - z) % 8 * wide, fields, 1)


def solution(mesh):
    wide = Mesh(mesh.devices.reshape(4, 2, 2, 4, 4), ("z_lo", "core", "z_hi", "x", "y"))
    whole = ("z_lo", "core", "z_hi", "x", "y")

    return jax.shard_map(
        body,
        mesh=wide,
        in_specs=(P(whole), P(whole), P(whole), P(whole), P(("z_lo", "core"))),
        out_specs=P(whole),
        check_vma=False,
    )
```

```python
import math

import jax
import jax.numpy as jnp
import numpy as np
from jax import lax
from jax.experimental import pallas as pl
from jax.experimental.pallas import tpu as pltpu
from jax.sharding import Mesh, PartitionSpec as P

GRID = 64
KYZ = 32
box_length = 10.0
screening = 1.0
epsilon = 1e-06
PLANE = ("core", "x", "y")
BLOCK = 8
YGRP = 8
HALF = 16
f32 = jnp.float32
bf16 = jnp.bfloat16


def real_basis(points, mode_count):
    cell = np.arange(points, dtype=np.float32)[:, None]
    mode = np.arange(mode_count, dtype=np.int32)[None, :]
    freq = (mode + 1) // 2
    phases = 2.0 * math.pi * cell * freq.astype(np.float32) / points
    values = np.where((mode % 2 == 1) | (mode == 0), np.cos(phases), np.sin(phases))
    factor = np.where((mode == 0) | (2 * freq == points), math.sqrt(1.0 / points), math.sqrt(2.0 / points))
    return (values * factor).astype(np.float32)


def coulomb_weights(half, weight):
    width = KYZ * HALF
    at = lax.broadcasted_iota(jnp.int32, (1, width), 1)
    freq_y = (((at >> 4) + 1) >> 1).astype(f32)
    freq_z = (((at & (HALF - 1)) + 1 + HALF * half) >> 1).astype(f32)
    plane = freq_y * freq_y + freq_z * freq_z
    for kx in range(GRID):
        square = plane + float(((kx + 1) // 2) ** 2)
        wave = (2.0 * math.pi / box_length) ** 2 * square
        weight[kx] = jnp.sqrt(4.0 * math.pi / (wave + screening * screening))


def spread(small, shape, row_of, col_of, keep):
    one_hot = lambda hit: jnp.where(hit, 1.0, 0.0).astype(bf16)
    iota = lambda dims, dim: lax.broadcasted_iota(jnp.int32, dims, dim)
    tall = (shape[0], small.shape[0])
    flat = (small.shape[1], shape[1])
    left = one_hot(row_of(iota(tall, 0)) == iota(tall, 1))
    right = one_hot(iota(flat, 0) == col_of(iota(flat, 1)))
    mid = jnp.dot(left, small, preferred_element_type=f32).astype(bf16)
    whole = jnp.dot(mid, right, preferred_element_type=f32)
    return jnp.where(keep(iota(shape, 0), iota(shape, 1)), whole, 0.0).astype(bf16)


def later_matrices(basis_x, basis_p, along_y, along_x):
    along_y[...] = spread(
        basis_p[...], along_y.shape, lambda r: r >> 4, lambda c: c >> 4, lambda r, c: (r & 15) == (c & 15)
    )
    along_x[...] = spread(
        basis_x[...], along_x.shape, lambda r: r >> 3, lambda c: c & 63, lambda r, c: (r & 7) == (c >> 6)
    )


def finish(first, along_y, along_x, weight, out):
    width = KYZ * HALF
    second = jnp.dot(first, along_y[...], preferred_element_type=f32).astype(bf16)
    piece = 256
    for n in range(width // piece):
        cols = slice(n * piece, (n + 1) * piece)
        g = jnp.dot(along_x[...], second[:, cols], preferred_element_type=f32)
        g = g.reshape(GRID, BLOCK, piece) * weight[:, :, cols]
        g = g.astype(bf16).reshape(GRID // 2, 2, BLOCK, piece)
        out[:, :, cols] = g[:, 0]
        out[:, :, width + n * piece : width + (n + 1) * piece] = g[:, 1]


def first_kernel(
    po, pv, occ_hbm, vir_hbm, basis_x, basis_p, out, rest, occ, vir, dens, first, along_z, along_y, along_x, weight, sems
):
    step = pl.program_id(0)

    @pl.when(step == 0)
    def _():
        loads = [
            pltpu.make_async_copy(occ_hbm, occ, sems.at[0]),
            pltpu.make_async_copy(vir_hbm, vir, sems.at[1]),
        ]
        for load in loads:
            load.start()
        along_z[...] = spread(
            basis_p[...],
            along_z.shape,
            lambda r: r & 63,
            lambda c: ((c >> 7) << 4) + (c & 15),
            lambda r, c: (r >> 6) == ((c & 127) >> 4),
        )
        later_matrices(basis_x, basis_p, along_y, along_x)
        coulomb_weights(0, weight)
        for load in loads:
            load.wait()

    tile_in = YGRP * GRID
    tile_out = YGRP * HALF
    for r in range(BLOCK):
        o = po[step * BLOCK + r]
        v = pv[step * BLOCK + r]
        dens[r * GRID : (r + 1) * GRID, :] = occ[o] * vir[v]
    for j in range(GRID // YGRP):
        t = jnp.dot(dens[:, j * tile_in : (j + 1) * tile_in], along_z[...], preferred_element_type=f32).astype(bf16)
        first[:, j * tile_out : (j + 1) * tile_out] = t[:, :tile_out]
        rest[:, j * tile_out : (j + 1) * tile_out] = t[:, tile_out:]
    finish(first[...], along_y, along_x, weight, out)


def second_kernel(first, basis_x, basis_p, out, along_y, along_x, weight):
    @pl.when(pl.program_id(0) == 0)
    def _():
        later_matrices(basis_x, basis_p, along_y, along_x)
        coulomb_weights(1, weight)

    finish(first[...], along_y, along_x, weight, out)


def make_gamma(occ, vir, pair_occ, pair_vir):
    pairs = pair_occ.shape[0]
    plane = KYZ * KYZ
    rows = BLOCK * GRID
    steps = pairs // BLOCK
    basis_x = jnp.asarray(real_basis(GRID, GRID).T).astype(bf16)
    basis_p = jnp.asarray(real_basis(GRID, KYZ)).astype(bf16)
    full = lambda shape: pl.BlockSpec(shape, lambda *at: (0,) * len(shape), pipeline_mode=pl.Buffered(1))
    half = pl.BlockSpec((GRID // 2, BLOCK, plane), lambda i, *_: (0, i, 0))
    part = pl.BlockSpec((rows, GRID * HALF), lambda i, *_: (i, 0))
    out_shape = jax.ShapeDtypeStruct((GRID // 2, pairs, plane), bf16)
    matrices = [
        pltpu.VMEM((GRID * HALF, KYZ * HALF), bf16),
        pltpu.VMEM((rows, rows), bf16),
        pltpu.VMEM((GRID, 1, KYZ * HALF), f32),
    ]
    front, rest = pl.pallas_call(
        first_kernel,
        out_shape=[out_shape, jax.ShapeDtypeStruct((pairs * GRID, GRID * HALF), bf16)],
        grid_spec=pltpu.PrefetchScalarGridSpec(
            num_scalar_prefetch=2,
            grid=(steps,),
            in_specs=[
                pl.BlockSpec(memory_space=pl.ANY),
                pl.BlockSpec(memory_space=pl.ANY),
                full(basis_x.shape),
                full(basis_p.shape),
            ],
            out_specs=[half, part],
            scratch_shapes=[
                pltpu.VMEM(occ.shape, bf16),
                pltpu.VMEM(vir.shape, bf16),
                pltpu.VMEM((rows, GRID * GRID), bf16),
                pltpu.VMEM((rows, GRID * HALF), bf16),
                pltpu.VMEM((YGRP * GRID, YGRP * KYZ), bf16),
                *matrices,
                pltpu.SemaphoreType.DMA((2,)),
            ],
        ),
        cost_estimate=pl.CostEstimate(flops=8_000_000_000, bytes_accessed=12_000_000, transcendentals=0),
        name="gamma_first",
    )(pair_occ, pair_vir, occ, vir, basis_x, basis_p)
    back = pl.pallas_call(
        second_kernel,
        out_shape=out_shape,
        grid_spec=pl.GridSpec(
            grid=(steps,),
            in_specs=[part, full(basis_x.shape), full(basis_p.shape)],
            out_specs=half,
            scratch_shapes=matrices,
        ),
        cost_estimate=pl.CostEstimate(flops=4_000_000_000, bytes_accessed=6_000_000, transcendentals=0),
        name="gamma_second",
    )(rest, basis_x, basis_p)
    return [front, back]


def ring_shift(value, by):
    place = lambda z: (z % 4) * 2 + z // 4
    return lax.ppermute(value, ("z_lo", "z_hi"), [(place(z), place((z + by) % 8)) for z in range(8)])


def exchange(value):
    return lax.all_to_all(value, PLANE, split_axis=0, concat_axis=0, tiled=True)


HEAD = 3
ROWS = 8


def body(occ_orbitals, vir_orbitals, pair_occ, pair_vir, sketch):
    pairs = pair_occ.shape[0]
    fields = sketch.shape[1]
    wide = fields // 8
    coef_count = GRID * KYZ * KYZ
    z = lax.axis_index("z_hi") * 4 + lax.axis_index("z_lo")

    gammas = make_gamma(occ_orbitals, vir_orbitals, pair_occ, pair_vir)
    got = [exchange(gammas[0]).reshape(32 * pairs, -1)]

    mine = sketch.reshape(2, -1, fields)[lax.axis_index("z_hi")]
    other = lax.ppermute(mine, "core", [(0, 1), (1, 0)])
    upper = lax.axis_index("core") == 0
    rows = jnp.concatenate([jnp.where(upper, mine, other), jnp.where(upper, other, mine)], axis=0)
    blocks = rows.T.reshape(8, wide, 32 * pairs)
    blocks = lax.dynamic_slice_in_dim(jnp.concatenate([blocks, blocks[:7]], axis=0), (z + HEAD) % 8, 8, 0)
    blocks = lax.optimization_barrier(blocks)

    squares = 0.0
    gathered = []
    for c in range(2):
        up = (3, 2, 1) if c == 0 else (4, 3, 2, 1)
        down = (4, 5, 6, 7) if c == 0 else (5, 6, 7)
        ahead = 2 if c == 0 else 3
        term = {}
        for at, to in ((0, ahead), (ahead, 8)):
            part = lax.dot_general(
                blocks[at:to].reshape((to - at) * wide, -1),
                got[c],
                (((1,), (0,)), ((), ())),
                preferred_element_type=f32,
            ).reshape(to - at, wide, -1)
            for i in range(at, to):
                term[(HEAD + i) % 8] = part[i - at]
            if c == 0 and at == 0:
                gammas[1], part = lax.optimization_barrier((gammas[1], part))
                got.append(exchange(gammas[1]).reshape(32 * pairs, -1))
        runs = {-1: term[down[0]].astype(bf16), 1: term[up[0]].astype(bf16)}
        for i in range(1, 4):
            for order, by in ((down, -1), (up, 1)):
                if i < len(order):
                    runs[by] = (ring_shift(runs[by], by).astype(f32) + term[order[i]]).astype(bf16)
            if c == 0 and i == 2:
                got[1] = lax.optimization_barrier((got[1], runs[1], runs[-1]))[0]
        total = term[0] + ring_shift(runs[-1], -1).astype(f32) + ring_shift(runs[1], 1).astype(f32)
        squares = squares + jnp.sum(jnp.square(total), axis=1)
        block = total.astype(bf16)
        if c == 1:
            high = squares.astype(bf16)
            low = (squares - high.astype(f32)).astype(bf16)
            tail = jnp.concatenate([high, low, jnp.zeros((block.shape[1] - 2 * wide,), bf16)])
            block = jnp.concatenate([block, jnp.broadcast_to(tail[None], (ROWS, block.shape[1]))], axis=0)
        held = {0: block}
        run = {-1: block, 1: block}
        for i in range(4):
            for by, hops in ((-1, 4 if c == 0 else 3), (1, 3 if c == 0 else 4)):
                if i < hops:
                    run[by] = ring_shift(run[by], by)
                    held[(-by * (i + 1)) % 8] = run[by]
        gathered.append(held)

    half = 16 * pairs
    place = lax.axis_index("core")

    def product(c, core):
        side = jnp.concatenate([gathered[c][k][:wide] for k in range(8)], axis=0)
        mine = lax.dynamic_slice_in_dim(got[c], core * half, half, 0)
        return lax.dot_general(mine, side, (((1,), (1,)), ((), ())), preferred_element_type=f32)

    early = product(0, 1 - place), product(0, place)
    early = lax.optimization_barrier(early)
    tails = [gathered[1][k][wide : wide + 1, : 2 * wide] for k in range(8)]
    sums = jnp.concatenate([t[:, :wide] for t in tails], axis=1), jnp.concatenate([t[:, wide:] for t in tails], axis=1)
    sums = jnp.concatenate([*sums, jnp.zeros((ROWS - 2, fields), bf16)], axis=0)
    away = (product(1, 1 - place) + early[0]).astype(bf16)
    away = lax.ppermute(jnp.concatenate([away, sums], axis=0), "core", [(0, 1), (1, 0)])
    near = product(1, place) + early[1]
    both = (near.astype(f32) + away[:half].astype(f32)).astype(bf16).reshape(16, pairs, fields)
    total = sums.astype(f32) + away[half:].astype(f32)
    total = total[:1] + total[1:2]
    high = total.astype(bf16)
    low = (total - high.astype(f32)).astype(bf16)
    total = jnp.concatenate([high, low, jnp.zeros((ROWS - 2, fields), bf16)], axis=0)
    both = jnp.concatenate([both, jnp.broadcast_to(total[None], (16, ROWS, fields))], axis=1)
    shares = lax.all_to_all(both, ("x", "y"), split_axis=0, concat_axis=0, tiled=True)
    shares = jnp.sum(shares.astype(f32), axis=0)
    scale = lax.rsqrt((shares[pairs : pairs + 1] + shares[pairs + 1 : pairs + 2]) / coef_count + epsilon)
    rolled = shares[:pairs] * (scale * (1.0 / math.sqrt(coef_count)))
    rolled = jnp.concatenate([rolled, rolled], axis=1)
    return lax.dynamic_slice_in_dim(rolled, (8 - z) % 8 * wide, fields, 1)


def solution(mesh):
    wide = Mesh(mesh.devices.reshape(4, 2, 2, 4, 4), ("z_lo", "core", "z_hi", "x", "y"))
    whole = ("z_lo", "core", "z_hi", "x", "y")

    return jax.shard_map(
        body,
        mesh=wide,
        in_specs=(P(whole), P(whole), P(whole), P(whole), P(("z_lo", "core"))),
        out_specs=P(whole),
        check_vma=False,
    )
```
